512 devices in a mesh: gx: 32 (over x_hi, y, core), gy: 16 (over z, x_lo).
Axes of the slice: x: 4 (x_hi: 2, x_lo: 2; x = x_hi * 2 + x_lo), y: 8, z: 8, core: 2. Of those that a mesh axis runs over, the one named last changes fastest.
Arguments:
- node_features: bfloat16 [64, 32, 64, 512], P('gx', 'gy'), may hold values from -6 to 6
- edge_features: bfloat16 [3, 64, 32, 64, 512], P(None, 'gx', 'gy'), may hold values from -6 to 6
- open_faces: int32 [3, 64, 32, 64], P(None, 'gx', 'gy'), may hold values 0 or 1
- edge_weight: bfloat16 [1536, 512], replicated, may hold values from -0.15625 to 0.15625
- node_weight: bfloat16 [512, 512], replicated, may hold values from -0.25 to 0.25
- cotangent: bfloat16 [64, 32, 64, 512], P('gx', 'gy'), may hold values from -6 to 6
Outputs:
- new_nodes: bfloat16 [64, 32, 64, 512], P('gx', 'gy')
- node_grad: bfloat16 [64, 32, 64, 512], P('gx', 'gy')
- edge_weight_grad: float32 [786432], P(('gx', 'gy'))
- node_weight_grad: float32 [262144], P(('gx', 'gy'))
The draws below stay inside these ranges and needn't reach their ends.
All inputs are finite; a program needn't handle non-finite values. No bound on the sum of `open_faces` on one device may be relied on, other than what follows from the above.
Results may differ from the reference program's by a relative error of at most 0.013.
Values may be sent and summed in bfloat16 or wider, within the bound.
A program may use at most 64 MiB of HBM per device.

```python
import jax
import jax.numpy as jnp
from jax import lax

H = 512
NZ = 64
NX = 64
NY = 32


def with_ends(result, own_key, least, high):
    spot = [jax.random.randint(jax.random.fold_in(own_key, axis), (), 0, length) for axis, length in enumerate(result.shape)]
    longest = result.shape.index(max(result.shape))
    beside = spot[:longest] + [(spot[longest] + 1) % result.shape[longest]] + spot[longest + 1:]
    return result.at[tuple(spot)].set(least).at[tuple(beside)].set(high)


def spiked(drawn, own_key, source, target, shards_of, factor):
    owner, partner = [(jnp.arange(drawn.shape[position]) // (drawn.shape[position] // shards_of)).reshape([-1 if axis == position else 1 for axis in range(drawn.ndim)]) for position in (source, target)]
    chosen = jax.random.permutation(own_key, shards_of)[partner]
    strong = (owner == chosen) | (owner == (partner + shards_of // 2) % shards_of)
    return jnp.where(strong, factor * drawn, drawn)


def block_scale(key, extent, cuts, smallest, top_value):
    level = 1.0
    for axis_at, shards_of in cuts:
        draws = jax.random.uniform(jax.random.fold_in(jax.random.fold_in(key, 6), axis_at), (shards_of,), jnp.float32, smallest / len(cuts), top_value / len(cuts))
        level = level * jnp.repeat(jnp.exp(draws), extent[axis_at] // shards_of).reshape((-1,) + (1,) * (len(extent) - 1 - axis_at))
    return level


def scatter_about(rng, extent, spread, reach, split=(), dtype=jnp.bfloat16):
    result = jax.random.normal(rng, extent, jnp.float32) * spread
    if len(split) > 0:
        result = block_scale(rng, extent, split, -0.22, 0.18) * result
    return jnp.clip(result, min=-reach, max=reach).astype(dtype)


def heavy_noise(stream_key, extent, width, bound, shards, heavy, kind=jnp.bfloat16):
    entries = width * jax.random.normal(stream_key, extent, jnp.float32)
    if shards:
        entries = entries * block_scale(stream_key, extent, shards, -0.22, 0.18)
    return jnp.clip(spiked(entries, jax.random.fold_in(stream_key, 3), *heavy), -bound, bound).astype(kind)


def setup_inputs(seed: int = 0) -> dict:
    arg_keys = jax.random.split(jax.random.key(seed), 7)
    node_features = heavy_noise(arg_keys[0], (NX, NY, NZ, H), 1.0, 6.0, ((0, 32), (1, 16)), (0, 3, 32, 2.75))
    edge_features = heavy_noise(arg_keys[1], (3, NX, NY, NZ, H), 1.0, 6.0, ((1, 32), (2, 16)), (1, 4, 32, 2.75))
    open_faces = with_ends((jax.random.randint(arg_keys[2], (3, NX, NY, NZ), 0, 4) < 3).astype(jnp.int32), jax.random.fold_in(arg_keys[2], 1), 0, 1)
    edge_weight = scatter_about(arg_keys[3], (3 * H, H), (3 * H) ** -0.5, 0.15625)
    node_weight = scatter_about(arg_keys[4], (H, H), H ** -0.5, 0.25)
    cotangent = scatter_about(arg_keys[5], (NX, NY, NZ, H), 1.0, 6.0, ((0, 32), (1, 16)))
    return dict(node_features=node_features, edge_features=edge_features, open_faces=open_faces, edge_weight=edge_weight, node_weight=node_weight, cotangent=cotangent)


def silu_slope(values):
    sigmoid = jax.nn.sigmoid(values)
    return sigmoid * (1.0 + values * (1.0 - sigmoid))


def from_above(values, axis_dim):
    length = values.shape[axis_dim]
    trimmed = lax.slice_in_dim(values, 1, length, axis=axis_dim)
    padding = [(0, 0)] * values.ndim
    padding[axis_dim] = (0, 1)
    return jnp.pad(trimmed, padding)


def from_below(values, axis_dim):
    length = values.shape[axis_dim]
    trimmed = lax.slice_in_dim(values, 0, length - 1, axis=axis_dim)
    padding = [(0, 0)] * values.ndim
    padding[axis_dim] = (1, 0)
    return jnp.pad(trimmed, padding)


def rows_of(values):
    return values.reshape(-1, values.shape[-1])


def reference(node_features, edge_features, open_faces, edge_weight, node_weight, cotangent):
    features = node_features.shape[-1]
    shape = node_features.shape
    self_weight = edge_weight[:features]
    other_weight = edge_weight[features:2 * features]
    stored_weight = edge_weight[2 * features:]
    summed = jnp.zeros(shape, jnp.float32)
    preacts, neighbours, open_masks = [], [], []
    for direction in range(3):
        neighbour = from_above(node_features, direction)
        length = shape[direction]
        inside = (jnp.arange(length) < length - 1).astype(jnp.float32)
        broadcast_shape = [1, 1, 1]
        broadcast_shape[direction] = length
        open_mask = open_faces[direction].astype(jnp.float32) * inside.reshape(broadcast_shape)
        preact = (jnp.dot(rows_of(node_features), self_weight, preferred_element_type=jnp.float32)
                  + jnp.dot(rows_of(neighbour), other_weight, preferred_element_type=jnp.float32)
                  + jnp.dot(rows_of(edge_features[direction]), stored_weight, preferred_element_type=jnp.float32)).reshape(shape)
        message = (jax.nn.silu(preact) * open_mask[..., None]).astype(jnp.bfloat16)
        widened = message.astype(jnp.float32)
        summed = summed + widened - from_below(widened, direction)
        preacts.append(preact)
        neighbours.append(neighbour)
        open_masks.append(open_mask)
    summed_half = summed.astype(jnp.bfloat16)
    update = jnp.dot(rows_of(summed_half), node_weight, preferred_element_type=jnp.float32).reshape(shape)
    new_nodes = (node_features.astype(jnp.float32) + jax.nn.silu(update)).astype(jnp.bfloat16)
    grad_update = (cotangent.astype(jnp.float32) * silu_slope(update)).astype(jnp.bfloat16)
    node_weight_grad = jnp.dot(rows_of(summed_half).T, rows_of(grad_update), preferred_element_type=jnp.float32)
    grad_summed = jnp.dot(rows_of(grad_update), node_weight.T, preferred_element_type=jnp.float32).reshape(shape).astype(jnp.bfloat16)
    grad_wide = grad_summed.astype(jnp.float32)
    node_grad = cotangent.astype(jnp.float32)
    self_grad = jnp.zeros((features, features), jnp.float32)
    other_grad = jnp.zeros((features, features), jnp.float32)
    stored_grad = jnp.zeros((features, features), jnp.float32)
    for direction in range(3):
        grad_message = grad_wide - from_above(grad_wide, direction)
        grad_preact = (grad_message * open_masks[direction][..., None] * silu_slope(preacts[direction])).astype(jnp.bfloat16)
        flat_grad = rows_of(grad_preact)
        self_grad = self_grad + jnp.dot(rows_of(node_features).T, flat_grad, preferred_element_type=jnp.float32)
        other_grad = other_grad + jnp.dot(rows_of(neighbours[direction]).T, flat_grad, preferred_element_type=jnp.float32)
        stored_grad = stored_grad + jnp.dot(rows_of(edge_features[direction]).T, flat_grad, preferred_element_type=jnp.float32)
        own_term = jnp.dot(flat_grad, self_weight.T, preferred_element_type=jnp.float32).reshape(shape)
        upper_term = jnp.dot(flat_grad, other_weight.T, preferred_element_type=jnp.float32).reshape(shape)
        node_grad = node_grad + own_term + from_below(upper_term, direction)
    edge_weight_grad = jnp.concatenate([self_grad, other_grad, stored_grad], axis=0)
    return new_nodes, node_grad.astype(jnp.bfloat16), edge_weight_grad.reshape(-1), node_weight_grad.reshape(-1)
```

```python
import jax
import jax.numpy as jnp
from jax import lax
from jax.experimental import pallas as pl
from jax.experimental.pallas import tpu as pltpu
from jax.sharding import PartitionSpec as P


def passed_along(value, axis, steps):
    count = lax.axis_size(axis)
    first, last = (max(0, -steps), min(count, count - steps))
    return lax.ppermute(value, axis, [(source, source + steps) for source in range(first, last)])


def silu_slope(values):
    sigmoid = jax.nn.sigmoid(values)
    return sigmoid * (1.0 + values * (1.0 - sigmoid))


MESH = pl.DeviceIdType.MESH
BF = jnp.bfloat16
F32 = jnp.float32


class Place:
    def __init__(self):
        gx, gy = lax.axis_index("gx"), lax.axis_index("gy")
        self.gx, self.gy = gx, gy
        self.x_hi, self.y, self.core = gx // 16, (gx // 2) % 8, gx % 2
        self.z, self.x_lo = gy // 2, gy % 2
        self.x = self.x_hi * 2 + self.x_lo
        self.sibling = (gx + 1 - 2 * self.core, gy)

    def along(self, axis, step):
        if axis == "x":
            other = (self.x + step) % 4
            return other, ((other // 2) * 16 + self.y * 2 + self.core, self.z * 2 + other % 2)
        if axis == "y":
            other = (self.y + step) % 8
            return other, (self.x_hi * 16 + other * 2 + self.core, self.gy)
        other = (self.z + step) % 8
        return other, (self.gx, other * 2 + self.x_lo)

    def partners(self):
        found = [self.sibling]
        for axis, count in (("x", 4), ("y", 8), ("z", 8)):
            found += [self.along(axis, step)[1] for step in range(1, count)]
        return found


def greet(devices):
    barrier = pltpu.get_barrier_semaphore()
    for device in devices:
        pl.semaphore_signal(barrier, inc=1, device_id=device, device_id_type=MESH)
    pl.semaphore_wait(barrier, len(devices))


def push(source, target, send_sem, recv_sem, device):
    copy = pltpu.make_async_remote_copy(
        src_ref=source, dst_ref=target, send_sem=send_sem, recv_sem=recv_sem, device_id=device, device_id_type=MESH
    )
    copy.start()
    return copy


SIZES = {"x": 4, "y": 8, "z": 8}
FAR = {4: (2, 1, 3), 8: (4, 3, 5, 2, 6, 1, 7)}
ORDERS = (("x", "y", "z"), ("y", "x", "z"), ("z", "x", "y"), ("x", "z", "y"))
TYPES = {0: (0, 0), 1: (0, 1), 3: (1, 0), 2: (1, 1)}


def scatter_scratch():
    shapes = []
    for first, second, _ in ORDERS:
        one, two = SIZES[first], SIZES[second]
        shapes += [pltpu.VMEM((one, 2, two, 16, 128), BF)] * 2
        shapes += [pltpu.VMEM((two, 2, 16, 128), BF)] * 2
    shapes += [pltpu.VMEM((2, 64, 128), F32)]
    shapes += [pltpu.VMEM((2, 8, 8, 128), F32)] * 2
    shapes += [pltpu.VMEM((2, 8, 128), F32)] * 2
    shapes += [pltpu.SemaphoreType.DMA((4, 8))] * 4 + [pltpu.SemaphoreType.DMA((2, 8))] * 2
    shapes += [pltpu.SemaphoreType.DMA] * 2
    return shapes


def fill_first(place, plane, step, edge, node, out):
    first, second, _ = ORDERS[plane]
    dest, device = place.along(first, step)
    for c in range(2):
        if plane == 0:
            start = 768 * (dest // 2) + 3 * (dest % 2)
            rows = edge[c, pl.ds(start, 128, stride=6), :]
            out[step, c] = rows.astype(BF).reshape(8, 16, 128)
        elif plane == 1:
            for hi in range(2):
                for lo in range(2):
                    start = 768 * hi + 3 * lo + 1 + 96 * dest
                    out[step, c, 2 * hi + lo] = edge[c, pl.ds(start, 16, stride=6), :].astype(BF)
        elif plane == 2:
            for hi in range(2):
                for lo in range(2):
                    start = 768 * hi + 3 * lo + 2 + 6 * dest
                    rows = [edge[c, pl.ds(start + 48 * core, 8, stride=96), :] for core in range(2)]
                    out[step, c, 2 * hi + lo] = jnp.concatenate(rows, axis=0).astype(BF)
        else:
            for high in range(8):
                start = 256 * (dest // 2) + dest % 2 + 2 * high
                rows = [node[c, pl.ds(start + 16 * core, 8, stride=32), :] for core in range(2)]
                out[step, c, high] = jnp.concatenate(rows, axis=0).astype(BF)
    return device


def scatter(place, edge, node, scratch, planes_first=(1, 2, 0, 3)):
    bufs = [scratch[4 * plane: 4 * plane + 4] for plane in range(4)]
    wide, send_three, recv_three, last, last_in = scratch[16:21]
    send_1, recv_1, send_2, recv_2, send_3, recv_3, send_4, recv_4 = scratch[21:29]
    stage_1 = {plane: {} for plane in range(4)}
    stage_2 = {plane: {} for plane in range(4)}
    for plane in planes_first:
        first = ORDERS[plane][0]
        out, landing = bufs[plane][:2]
        for step in FAR[SIZES[first]]:
            device = fill_first(place, plane, step, edge, node, out)
            stage_1[plane][step] = push(out.at[step], landing.at[step], send_1.at[plane, step], recv_1.at[plane, step], device)
        fill_first(place, plane, 0, edge, node, out)
    for plane in planes_first:
        first, second, _ = ORDERS[plane]
        out, landing, out_2, landing_2 = bufs[plane]
        for step in (1, 7, 2, 6, 3, 5, 4) if SIZES[first] == 8 else (1, 3, 2):
            stage_1[plane][step].wait_recv()
        for step in FAR[SIZES[second]] + (0,):
            dest, device = place.along(second, step)
            total = out[0, :, dest].astype(F32)
            for source in range(1, SIZES[first]):
                total = total + landing[source, :, dest].astype(F32)
            out_2[step] = total.astype(BF)
            if step:
                stage_2[plane][step] = push(out_2.at[step], landing_2.at[step], send_2.at[plane, step], recv_2.at[plane, step], device)
    stage_3 = []
    for kind, axis in ((0, "z"), (1, "y")):
        for plane in range(4):
            if TYPES[plane][0] != kind:
                continue
            out_2, landing_2 = bufs[plane][2:]
            count = SIZES[ORDERS[plane][1]]
            for step in range(1, count):
                stage_2[plane][step].wait_recv()
            total = out_2[0].astype(F32)
            for source in range(1, count):
                total = total + landing_2[source].astype(F32)
            slot = TYPES[plane][1]
            for c in range(2):
                for core in range(2):
                    row = (core * 4 + slot * 2 + c) * 8
                    wide[kind, pl.ds(row, 8), :] = total[c, core * 8: core * 8 + 8]
        for step in FAR[8] + (0,):
            dest, device = place.along(axis, step)
            send_three[kind, step] = wide[kind, pl.ds(dest, 8, stride=8), :]
            if step:
                stage_3.append(push(send_three.at[kind, step], recv_three.at[kind, step], send_3.at[kind, step], recv_3.at[kind, step], device))
    for copy in stage_3:
        copy.wait_recv()
    for kind in range(2):
        total = send_three[kind, 0]
        for step in range(1, 8):
            total = total + recv_three[kind, step]
        last[kind] = total
    swap = push(last, last_in, send_4, recv_4, place.sibling)
    swap.wait_recv()
    pending = stage_3 + [swap]
    for plane in range(4):
        pending += list(stage_1[plane].values()) + list(stage_2[plane].values())

    def finish(edge_out, node_out):
        for plane in range(4):
            kind, slot = TYPES[plane]
            rows = pl.ds(place.core * 4 + slot * 2, 2)
            mine, theirs = last[kind, rows, :], last_in[kind, rows, :]
            low = jnp.where(place.core == 0, mine, theirs)
            high = jnp.where(place.core == 0, theirs, mine)
            if plane < 3:
                edge_out[pl.ds(4 * plane, 2), :] = low
                edge_out[pl.ds(4 * plane + 2, 2), :] = high
            else:
                node_out[pl.ds(0, 2), :] = low
                node_out[pl.ds(2, 2), :] = high
        for copy in pending:
            copy.wait_send()

    return finish


def reduce_kernel(edge_in, node_in, edge_out, node_out, edge, node, edge_to, edge_from, node_to, node_from, swap_send, swap_recv, *scratch):
    place = Place()
    mine = pl.multiple_of(place.core * 256, 256)
    other = pl.multiple_of(256 - place.core * 256, 256)
    greet(place.partners())
    node_to[...] = node_in[:, pl.ds(other, 256)].astype(BF)
    swaps = [push(node_to, node_from, swap_send.at[3], swap_recv.at[3], place.sibling)]
    for part in range(3):
        rows = pl.ds(512 * part, 512)
        edge_to[part] = edge_in[rows, pl.ds(other, 256)].astype(BF)
        swaps.append(push(edge_to.at[part], edge_from.at[part], swap_send.at[part], swap_recv.at[part], place.sibling))
    swaps[0].wait_recv()
    for c in range(2):
        node[c] = node_in[:, pl.ds(pl.multiple_of(mine + 128 * c, 128), 128)] + node_from[:, 128 * c: 128 * c + 128].astype(F32)
    for part in range(3):
        swaps[part + 1].wait_recv()
        for c in range(2):
            edge[c, pl.ds(512 * part, 512), :] = edge_in[pl.ds(512 * part, 512), pl.ds(pl.multiple_of(mine + 128 * c, 128), 128)] + edge_from[part, :, 128 * c: 128 * c + 128].astype(F32)
    finish = scatter(place, edge, node, scratch)
    finish(edge_out, node_out)
    for copy in swaps:
        copy.wait_send()


def reduce_scatter(edge_grad, node_grad):
    vmem = pl.BlockSpec(memory_space=pltpu.VMEM)
    edge_part, node_part = pl.pallas_call(
        reduce_kernel,
        out_shape=(jax.ShapeDtypeStruct((12, 128), F32), jax.ShapeDtypeStruct((4, 128), F32)),
        in_specs=[vmem, vmem],
        out_specs=(vmem, vmem),
        scratch_shapes=[
            pltpu.VMEM((2, 1536, 128), F32),
            pltpu.VMEM((2, 512, 128), F32),
            pltpu.VMEM((3, 512, 256), BF),
            pltpu.VMEM((3, 512, 256), BF),
            pltpu.VMEM((512, 256), BF),
            pltpu.VMEM((512, 256), BF),
            pltpu.SemaphoreType.DMA((4,)),
            pltpu.SemaphoreType.DMA((4,)),
        ] + scatter_scratch(),
        compiler_params=pltpu.CompilerParams(collective_id=0, has_side_effects=True, vmem_limit_bytes=40 * 1024 * 1024),
        name="reduce_scatter",
    )(edge_grad, node_grad)
    return edge_part.reshape(-1), node_part.reshape(-1)


def local(node_features, edge_features, open_faces, edge_weight, node_weight, cotangent):
    extent_first, extent_second, depth, features = node_features.shape
    total_first = extent_first * lax.axis_size("gx")
    total_second = extent_second * lax.axis_size("gy")
    place_first = lax.axis_index("gx") * extent_first + jnp.arange(extent_first)
    place_second = lax.axis_index("gy") * extent_second + jnp.arange(extent_second)
    inside_first = (place_first < total_first - 1).astype(jnp.float32)
    inside_second = (place_second < total_second - 1).astype(jnp.float32)
    inside_third = (jnp.arange(depth) < depth - 1).astype(jnp.float32)
    masks = open_faces.astype(jnp.float32)
    open_first = masks[0] * inside_first[:, None, None]
    open_second = masks[1] * inside_second[None, :, None]
    open_third = masks[2] * inside_third[None, None, :]
    open_all = jnp.stack([open_first, open_second, open_third])
    upper_first = passed_along(node_features[0:1], "gx", -1)
    upper_second = passed_along(node_features[:, 0:1], "gy", -1)
    zero_plane = jnp.zeros((extent_first, extent_second, 1, features), jnp.bfloat16)
    beside = [
        jnp.concatenate([node_features[1:], upper_first], axis=0),
        jnp.concatenate([node_features[:, 1:], upper_second], axis=1),
        jnp.concatenate([node_features[:, :, 1:], zero_plane], axis=2),
    ]
    inputs_all = jnp.concatenate(
        [
            jnp.concatenate([node_features, beside[direction], edge_features[direction]], axis=-1)
            for direction in range(3)
        ],
        axis=0,
    )
    flat_inputs = inputs_all.reshape(-1, 3 * features)
    preact = jnp.dot(flat_inputs, edge_weight, preferred_element_type=jnp.float32)
    preact = preact.reshape(3, extent_first, extent_second, depth, features)
    message = (jax.nn.silu(preact) * open_all[..., None]).astype(jnp.bfloat16)
    widened = message.astype(jnp.float32)
    zero_wide = jnp.zeros((extent_first, extent_second, 1, features), jnp.float32)
    summed = widened[0] + widened[1] + widened[2]
    summed = summed - jnp.concatenate([zero_wide, widened[2, :, :, :-1]], axis=2)
    from_first = passed_along(message[0, -1:], "gx", 1)
    from_second = passed_along(message[1, :, -1:], "gy", 1)
    entering_first = from_first.astype(jnp.float32)
    entering_second = from_second.astype(jnp.float32)
    summed = summed - jnp.concatenate([entering_first, widened[0, :-1]], axis=0)
    summed = summed - jnp.concatenate([entering_second, widened[1, :, :-1]], axis=1)
    summed_half = summed.astype(jnp.bfloat16)
    flat_summed = summed_half.reshape(-1, features)
    update = jnp.dot(flat_summed, node_weight, preferred_element_type=jnp.float32).reshape(
        node_features.shape
    )
    new_nodes = (node_features.astype(jnp.float32) + jax.nn.silu(update)).astype(jnp.bfloat16)
    grad_update = (cotangent.astype(jnp.float32) * silu_slope(update)).astype(jnp.bfloat16)
    flat_update = grad_update.reshape(-1, features)
    node_weight_grad = lax.dot_general(
        flat_summed, flat_update, (((0,), (0,)), ((), ())), preferred_element_type=jnp.float32
    )
    grad_summed = lax.dot_general(
        flat_update, node_weight, (((1,), (1,)), ((), ())), preferred_element_type=jnp.float32
    )
    grad_summed = grad_summed.reshape(node_features.shape).astype(jnp.bfloat16)
    grad_upper_first = passed_along(grad_summed[0:1], "gx", -1)
    grad_upper_second = passed_along(grad_summed[:, 0:1], "gy", -1)
    beside_grad = jnp.stack(
        [
            jnp.concatenate([grad_summed[1:], grad_upper_first], axis=0),
            jnp.concatenate([grad_summed[:, 1:], grad_upper_second], axis=1),
            jnp.concatenate([grad_summed[:, :, 1:], zero_plane], axis=2),
        ]
    )
    grad_message = grad_summed.astype(jnp.float32)[None] - beside_grad.astype(jnp.float32)
    grad_preact = (grad_message * open_all[..., None] * silu_slope(preact)).astype(jnp.bfloat16)
    flat_grad = grad_preact.reshape(-1, features)
    edge_weight_grad = lax.dot_general(
        flat_inputs, flat_grad, (((0,), (0,)), ((), ())), preferred_element_type=jnp.float32
    )
    backward = lax.dot_general(
        flat_grad,
        edge_weight[: 2 * features],
        (((1,), (1,)), ((), ())),
        preferred_element_type=jnp.float32,
    )
    backward = backward.reshape(3, extent_first, extent_second, depth, 2 * features)
    own_terms = backward[..., :features]
    toward = backward[..., features:]
    node_grad = cotangent.astype(jnp.float32) + own_terms[0] + own_terms[1] + own_terms[2]
    node_grad = node_grad + jnp.concatenate([zero_wide, toward[2, :, :, :-1]], axis=2)
    lower_first = passed_along(toward[0, -1:].astype(jnp.bfloat16), "gx", 1).astype(jnp.float32)
    lower_second = passed_along(toward[1, :, -1:].astype(jnp.bfloat16), "gy", 1).astype(jnp.float32)
    node_grad = node_grad + jnp.concatenate([lower_first, toward[0, :-1]], axis=0)
    node_grad = node_grad + jnp.concatenate([lower_second, toward[1, :, :-1]], axis=1)
    edge_part, node_part = reduce_scatter(edge_weight_grad, node_weight_grad)
    return (new_nodes, node_grad.astype(jnp.bfloat16), edge_part, node_part)


def solution(mesh):
    placed = (
        P("gx", "gy", None, None),
        P(None, "gx", "gy", None, None),
        P(None, "gx", "gy", None),
        P(),
        P(),
        P("gx", "gy", None, None),
    )
    return jax.shard_map(
        local,
        mesh=mesh,
        in_specs=placed,
        out_specs=(
            P("gx", "gy", None, None),
            P("gx", "gy", None, None),
            P(("gx", "gy")),
            P(("gx", "gy")),
        ),
        check_vma=False,
    )
```

```python
import jax
import jax.numpy as jnp
from jax import lax
from jax.experimental import pallas as pl
from jax.experimental.pallas import tpu as pltpu
from jax.sharding import PartitionSpec as P

MESH = pl.DeviceIdType.MESH
BF = jnp.bfloat16
F32 = jnp.float32


class Place:
    def __init__(self):
        gx, gy = lax.axis_index("gx"), lax.axis_index("gy")
        self.gx, self.gy = gx, gy
        self.x_hi, self.y, self.core = gx // 16, (gx // 2) % 8, gx % 2
        self.z, self.x_lo = gy // 2, gy % 2
        self.x = self.x_hi * 2 + self.x_lo
        self.sibling = (gx + 1 - 2 * self.core, gy)

    def along(self, axis, step):
        if axis == "x":
            other = (self.x + step) % 4
            return other, ((other // 2) * 16 + self.y * 2 + self.core, self.z * 2 + other % 2)
        if axis == "y":
            other = (self.y + step) % 8
            return other, (self.x_hi * 16 + other * 2 + self.core, self.gy)
        other = (self.z + step) % 8
        return other, (self.gx, other * 2 + self.x_lo)

    def beside(self, first, second):
        return ((self.gx + first) % 32, (self.gy + second) % 16)

    def partners(self):
        found = [self.sibling, self.beside(1, 0), self.beside(-1, 0), self.beside(0, 1), self.beside(0, -1)]
        for axis, count in (("x", 4), ("y", 8), ("z", 8)):
            found += [self.along(axis, step)[1] for step in range(1, count)]
        return found


def greet(devices, meanwhile):
    barrier = pltpu.get_barrier_semaphore()
    for device in devices:
        pl.semaphore_signal(barrier, inc=1, device_id=device, device_id_type=MESH)
    meanwhile()
    pl.semaphore_wait(barrier, len(devices))


def push(source, target, send_sem, recv_sem, device):
    copy = pltpu.make_async_remote_copy(
        src_ref=source, dst_ref=target, send_sem=send_sem, recv_sem=recv_sem, device_id=device, device_id_type=MESH
    )
    copy.start()
    return copy


SIZES = {"x": 4, "y": 8, "z": 8}
FAR = {4: (2, 1, 3), 8: (4, 3, 5, 2, 6, 1, 7)}
ORDERS = (("x", "y", "z"), ("y", "x", "z"), ("z", "x", "y"), ("x", "z", "y"))
TYPES = {0: (0, 0), 1: (0, 1), 3: (1, 0), 2: (1, 1)}


def scatter_scratch():
    shapes = []
    for first, second, _ in ORDERS:
        one, two = SIZES[first], SIZES[second]
        shapes += [pltpu.VMEM((one, 2, two, 16, 128), BF)] * 2
        shapes += [pltpu.VMEM((two, 2, 16, 128), BF)] * 2
    shapes += [pltpu.VMEM((2, 64, 128), F32)]
    shapes += [pltpu.VMEM((2, 8, 8, 128), F32)] * 2
    shapes += [pltpu.VMEM((2, 8, 128), F32)] * 2
    shapes += [pltpu.SemaphoreType.DMA((4, 8))] * 4 + [pltpu.SemaphoreType.DMA((2, 8))] * 2
    shapes += [pltpu.SemaphoreType.DMA] * 2
    return shapes


def fill_first(place, plane, step, edge, node, out):
    first, second, _ = ORDERS[plane]
    dest, device = place.along(first, step)
    for c in range(2):
        if plane == 0:
            start = 768 * (dest // 2) + 3 * (dest % 2)
            rows = edge[c, pl.ds(start, 128, stride=6), :]
            out[step, c] = rows.astype(BF).reshape(8, 16, 128)
        elif plane == 1:
            for hi in range(2):
                for lo in range(2):
                    start = 768 * hi + 3 * lo + 1 + 96 * dest
                    out[step, c, 2 * hi + lo] = edge[c, pl.ds(start, 16, stride=6), :].astype(BF)
        elif plane == 2:
            for hi in range(2):
                for lo in range(2):
                    start = 768 * hi + 3 * lo + 2 + 6 * dest
                    rows = [edge[c, pl.ds(start + 48 * core, 8, stride=96), :] for core in range(2)]
                    out[step, c, 2 * hi + lo] = jnp.concatenate(rows, axis=0).astype(BF)
        else:
            for high in range(8):
                start = 256 * (dest // 2) + dest % 2 + 2 * high
                rows = [node[c, pl.ds(start + 16 * core, 8, stride=32), :] for core in range(2)]
                out[step, c, high] = jnp.concatenate(rows, axis=0).astype(BF)
    return device


def scatter(place, edge, node, scratch, meanwhile, planes_first=(1, 2, 0, 3)):
    bufs = [scratch[4 * plane: 4 * plane + 4] for plane in range(4)]
    wide, send_three, recv_three, last, last_in = scratch[16:21]
    send_1, recv_1, send_2, recv_2, send_3, recv_3, send_4, recv_4 = scratch[21:29]
    stage_1 = {plane: {} for plane in range(4)}
    stage_2 = {plane: {} for plane in range(4)}
    for plane in planes_first:
        first = ORDERS[plane][0]
        out, landing = bufs[plane][:2]
        for step in FAR[SIZES[first]]:
            device = fill_first(place, plane, step, edge, node, out)
            stage_1[plane][step] = push(out.at[step], landing.at[step], send_1.at[plane, step], recv_1.at[plane, step], device)
        fill_first(place, plane, 0, edge, node, out)
    meanwhile()
    for plane in planes_first:
        first, second, _ = ORDERS[plane]
        out, landing, out_2, landing_2 = bufs[plane]
        for step in (1, 7, 2, 6, 3, 5, 4) if SIZES[first] == 8 else (1, 3, 2):
            stage_1[plane][step].wait_recv()
        for step in FAR[SIZES[second]] + (0,):
            dest, device = place.along(second, step)
            total = out[0, :, dest].astype(F32)
            for source in range(1, SIZES[first]):
                total = total + landing[source, :, dest].astype(F32)
            out_2[step] = total.astype(BF)
            if step:
                stage_2[plane][step] = push(out_2.at[step], landing_2.at[step], send_2.at[plane, step], recv_2.at[plane, step], device)
    stage_3 = []
    for kind, axis in ((0, "z"), (1, "y")):
        for plane in range(4):
            if TYPES[plane][0] != kind:
                continue
            out_2, landing_2 = bufs[plane][2:]
            count = SIZES[ORDERS[plane][1]]
            for step in range(1, count):
                stage_2[plane][step].wait_recv()
            total = out_2[0].astype(F32)
            for source in range(1, count):
                total = total + landing_2[source].astype(F32)
            slot = TYPES[plane][1]
            for c in range(2):
                for core in range(2):
                    row = (core * 4 + slot * 2 + c) * 8
                    wide[kind, pl.ds(row, 8), :] = total[c, core * 8: core * 8 + 8]
        for step in FAR[8] + (0,):
            dest, device = place.along(axis, step)
            send_three[kind, step] = wide[kind, pl.ds(dest, 8, stride=8), :]
            if step:
                stage_3.append(push(send_three.at[kind, step], recv_three.at[kind, step], send_3.at[kind, step], recv_3.at[kind, step], device))
    for copy in stage_3:
        copy.wait_recv()
    for kind in range(2):
        total = send_three[kind, 0]
        for step in range(1, 8):
            total = total + recv_three[kind, step]
        last[kind] = total
    swap = push(last, last_in, send_4, recv_4, place.sibling)
    swap.wait_recv()
    pending = stage_3 + [swap]
    for plane in range(4):
        pending += list(stage_1[plane].values()) + list(stage_2[plane].values())

    def finish(edge_out, node_out):
        for plane in range(4):
            kind, slot = TYPES[plane]
            rows = pl.ds(place.core * 4 + slot * 2, 2)
            mine, theirs = last[kind, rows, :], last_in[kind, rows, :]
            low = jnp.where(place.core == 0, mine, theirs)
            high = jnp.where(place.core == 0, theirs, mine)
            if plane < 3:
                edge_out[pl.ds(4 * plane, 2), :] = low
                edge_out[pl.ds(4 * plane + 2, 2), :] = high
            else:
                node_out[pl.ds(0, 2), :] = low
                node_out[pl.ds(2, 2), :] = high
        for copy in pending:
            copy.wait_send()

    return finish


def mul(left, right):
    return jnp.dot(left, right, preferred_element_type=F32)


def mul_nt(left, right):
    return lax.dot_general(left, right, (((1,), (1,)), ((), ())), preferred_element_type=F32)


def mul_tn(left, right):
    return lax.dot_general(left, right, (((0,), (0,)), ((), ())), preferred_element_type=F32)


def sigmoid(value):
    return 0.5 + 0.5 * jnp.tanh(0.5 * value)


BLOCKS = ((0, 0), (0, 1), (1, 0), (1, 1))


def step_kernel(nf_in, ef_in, faces_in, we_in, wn_in, cot_in, nn_out, ng_out, edge_out, node_out,
                nf, ef, faces, we, wn, cot, spread, masks, pre, self_part, upper_part,
                halo_x, halo_y, msg, in_x, in_y, summed, gu, gs, gs_x, gs_y, gp, gp_x, gp_y, gsum, tsum,
                nf_t, hx_t, hy_t, ef_t, nn, ng, load_sem, store_sem, halo_send, halo_recv,
                edge, node, edge_to, edge_from, node_to, node_from, swap_send, swap_recv, *scratch):
    place = Place()
    mine = pl.multiple_of(place.core * 256, 256)
    other = pl.multiple_of(256 - place.core * 256, 256)
    loads = []

    def load():
        for index, (source, target) in enumerate(((nf_in, nf), (we_in, we), (ef_in, ef), (faces_in, faces), (wn_in, wn), (cot_in, cot))):
            copy = pltpu.make_async_copy(source, target, load_sem.at[index])
            copy.start()
            loads.append(copy)

    greet(place.partners(), load)
    down_x, up_x = place.beside(-1, 0), place.beside(1, 0)
    down_y, up_y = place.beside(0, -1), place.beside(0, 1)
    halos = {}

    def trade(index, source, target, device):
        halos[index] = push(source, target, halo_send.at[index], halo_recv.at[index], device)

    trade(1, nf_in.at[:, 0], halo_y, down_y)
    trade(0, nf_in.at[0], halo_x, down_x)

    loads[3].wait()
    spread[...] = jnp.zeros_like(spread)
    inside_x = jnp.where(place.gx < 31, 1.0, 0.0)
    inside_y = jnp.where(place.gy < 15, 1.0, 0.0)
    depth = lax.broadcasted_iota(jnp.int32, (2, 64), 1)
    second = lax.broadcasted_iota(jnp.int32, (2, 64), 0)
    for a in range(2):
        rows = faces[0, a].astype(F32)
        spread[pl.ds(2 * a, 2), :] = rows * inside_x if a else rows
        rows = faces[1, a].astype(F32)
        spread[pl.ds(4 + 2 * a, 2), :] = jnp.where(second == 1, rows * inside_y, rows)
        rows = faces[2, a].astype(F32)
        spread[pl.ds(8 + 2 * a, 2), :] = jnp.where(depth < 63, rows, 0.0)
    eye = lax.broadcasted_iota(jnp.int32, (64, 64), 0) == lax.broadcasted_iota(jnp.int32, (64, 64), 1)
    for row in range(12):
        column = jnp.where(eye, jnp.broadcast_to(spread[pl.ds(row, 1), :], (64, 64)), 0.0)
        masks[row] = jnp.broadcast_to(jnp.sum(column, axis=1, keepdims=True), (64, 128))

    loads[0].wait()
    loads[1].wait()
    own = nf[...].reshape(256, 512)
    self_part[...] = mul(own, we[0:512, :]).reshape(2, 2, 64, 512)
    upper_part[...] = mul(own, we[512:1024, :]).reshape(2, 2, 64, 512)
    loads[2].wait()
    for d in (2, 1, 0):
        stored = mul(ef[d].reshape(256, 512), we[1024:1536, :]).reshape(2, 2, 64, 512)
        pre[d] = stored + self_part[...]

    def edge_block(d, a, b, upper):
        mask = jnp.concatenate([masks[4 * d + 2 * a + b]] * 4, axis=1)
        value = pre[d, a, b] + upper
        s = sigmoid(value)
        msg[d, a, b] = (value * s * mask).astype(BF)
        pre[d, a, b] = mask * (s * (1.0 + value * (1.0 - s)))

    @pl.loop(0, 2)
    def _(a):
        for b in range(2):
            edge_block(2, a, b, pltpu.roll(upper_part[a, b], 63, 0))
        edge_block(0, 0, a, upper_part[1, a])
        edge_block(1, a, 0, upper_part[a, 1])

    nf_t[...] = own.T

    halos[1].wait_recv()
    self_part[0] = mul(halo_y[...].reshape(128, 512), we[512:1024, :]).reshape(2, 64, 512)
    @pl.loop(0, 2)
    def _(a):
        edge_block(1, a, 1, self_part[0, a])

    trade(3, msg.at[1, :, 1], in_y, up_y)
    halos[0].wait_recv()
    self_part[1] = mul(halo_x[...].reshape(128, 512), we[512:1024, :]).reshape(2, 64, 512)
    @pl.loop(0, 2)
    def _(b):
        edge_block(0, 1, b, self_part[1, b])

    trade(2, msg.at[0, 1], in_x, up_x)

    for d in range(3):
        ef_t[:, 256 * d: 256 * d + 256] = ef[d].reshape(256, 512).T
    hx_t[...] = halo_x[...].reshape(128, 512).T
    hy_t[...] = halo_y[...].reshape(128, 512).T
    loads[4].wait()
    loads[5].wait()

    halos[3].wait_recv()
    halos[2].wait_recv()
    for a, b in BLOCKS:
        third = msg[2, a, b].astype(F32)
        total = msg[0, a, b].astype(F32) + msg[1, a, b].astype(F32) + third
        total = total - pltpu.roll(third, 1, 0)
        total = total - (in_x[b] if a == 0 else msg[0, 0, b]).astype(F32)
        total = total - (in_y[a] if b == 0 else msg[1, a, 0]).astype(F32)
        summed[pl.ds(128 * a + 64 * b, 64), :] = total.astype(BF)
    upper_part[...] = mul(summed[...], wn[...]).reshape(2, 2, 64, 512)
    @pl.loop(0, 4)
    def _(block):
        a, b = block // 2, block % 2
        value = upper_part[a, b]
        s = sigmoid(value)
        nn[a, b] = (nf[a, b].astype(F32) + value * s).astype(BF)
        rows = pl.ds(pl.multiple_of(64 * block, 64), 64)
        gu[rows, :] = (cot[a, b].astype(F32) * (s * (1.0 + value * (1.0 - s)))).astype(BF)

    gs[...] = mul_nt(gu[...], wn[...]).astype(BF).reshape(2, 2, 64, 512)
    trade(5, gs.at[:, 0], gs_y, down_y)
    trade(4, gs.at[0], gs_x, down_x)
    store_nn = pltpu.make_async_copy(nn, nn_out, store_sem.at[0])
    store_nn.start()

    node_to[...] = mul_tn(summed[...], gu[:, pl.ds(other, 256)]).astype(BF)
    swaps = [push(node_to, node_from, swap_send.at[3], swap_recv.at[3], place.sibling)]
    for c in range(2):
        node[c] = mul_tn(summed[...], gu[:, pl.ds(pl.multiple_of(mine + 128 * c, 128), 128)])

    def grad_block(d, a, b, above):
        gp[d, a, b] = ((gs[a, b].astype(F32) - above) * pre[d, a, b]).astype(BF)

    for a, b in BLOCKS:
        grad_block(2, a, b, pltpu.roll(gs[a, b].astype(F32), 63, 0))
    for b in range(2):
        grad_block(0, 0, b, gs[1, b].astype(F32))
    for a in range(2):
        grad_block(1, a, 0, gs[a, 1].astype(F32))
    swaps[0].wait_recv()
    for c in range(2):
        node[c] = node[c] + node_from[:, 128 * c: 128 * c + 128].astype(F32)
    halos[5].wait_recv()
    for a in range(2):
        grad_block(1, a, 1, gs_y[a].astype(F32))
    trade(7, gp.at[1, :, 1], gp_y, up_y)
    halos[4].wait_recv()
    for b in range(2):
        grad_block(0, 1, b, gs_x[b].astype(F32))
    trade(6, gp.at[0, 1], gp_x, up_x)
    for a, b in BLOCKS:
        rows = pl.ds(128 * a + 64 * b, 64)
        third = gp[2, a, b].astype(F32)
        gsum[rows, :] = (gp[0, a, b].astype(F32) + gp[1, a, b].astype(F32) + third).astype(BF)
        total = pltpu.roll(third, 1, 0)
        if a:
            total = total + gp[0, 0, b].astype(F32)
        if b:
            total = total + gp[1, a, 0].astype(F32)
        tsum[rows, :] = total.astype(BF)

    def grads(part, columns):
        if part == 0:
            return mul(nf_t[...], gsum[:, columns])
        if part == 1:
            total = mul(nf_t[...], tsum[:, columns])
            total = total + mul(hx_t[...], gp[0, 1, :, :, columns].reshape(128, 256))
            return total + mul(hy_t[...], gp[1, :, 1, :, columns].reshape(128, 256))
        return mul(ef_t[...], gp[:, :, :, :, columns].reshape(768, 256))

    for part in range(3):
        edge_to[part] = grads(part, pl.ds(other, 256)).astype(BF)
        swaps.append(push(edge_to.at[part], edge_from.at[part], swap_send.at[part], swap_recv.at[part], place.sibling))
    for part in range(3):
        total = grads(part, pl.ds(mine, 256))
        for c in range(2):
            edge[c, pl.ds(512 * part, 512), :] = total[:, 128 * c: 128 * c + 128]
    for part in range(3):
        swaps[part + 1].wait_recv()
        for c in range(2):
            rows = pl.ds(512 * part, 512)
            edge[c, rows, :] = edge[c, rows, :] + edge_from[part, :, 128 * c: 128 * c + 128].astype(F32)

    def node_grads():
        halos[6].wait_recv()
        halos[7].wait_recv()
        for a, b in BLOCKS:
            total = pltpu.roll(gp[2, a, b].astype(F32), 1, 0)
            total = total + (gp[0, 0, b] if a else gp_x[b]).astype(F32)
            total = total + (gp[1, a, 0] if b else gp_y[a]).astype(F32)
            tsum[pl.ds(128 * a + 64 * b, 64), :] = total.astype(BF)
        upper_part[...] = (mul_nt(gsum[...], we[0:512, :]) + mul_nt(tsum[...], we[512:1024, :])).reshape(2, 2, 64, 512)

        @pl.loop(0, 4)
        def _(block):
            a, b = block // 2, block % 2
            ng[a, b] = (cot[a, b].astype(F32) + upper_part[a, b]).astype(BF)

        pltpu.make_async_copy(ng, ng_out, store_sem.at[1]).start()

    finish = scatter(place, edge, node, scratch, node_grads)
    finish(edge_out, node_out)
    for copy in swaps + list(halos.values()):
        copy.wait_send()
    store_nn.wait()
    pltpu.make_async_copy(ng, ng_out, store_sem.at[1]).wait()


def local(node_features, edge_features, open_faces, edge_weight, node_weight, cotangent):
    anywhere = pl.BlockSpec(memory_space=pltpu.HBM)
    vmem = pl.BlockSpec(memory_space=pltpu.VMEM)
    nodes = (2, 2, 64, 512)
    plane = (2, 64, 512)
    new_nodes, node_grad, edge_part, node_part = pl.pallas_call(
        step_kernel,
        out_shape=(
            jax.ShapeDtypeStruct(nodes, BF),
            jax.ShapeDtypeStruct(nodes, BF),
            jax.ShapeDtypeStruct((12, 128), F32),
            jax.ShapeDtypeStruct((4, 128), F32),
        ),
        in_specs=[anywhere] * 6,
        out_specs=(anywhere, anywhere, vmem, vmem),
        scratch_shapes=[
            pltpu.VMEM(nodes, BF),
            pltpu.VMEM((3,) + nodes, BF),
            pltpu.VMEM((3, 2, 2, 64), jnp.int32),
            pltpu.VMEM((1536, 512), BF),
            pltpu.VMEM((512, 512), BF),
            pltpu.VMEM(nodes, BF),
            pltpu.VMEM((16, 64), F32),
            pltpu.VMEM((12, 64, 128), F32),
            pltpu.VMEM((3,) + nodes, F32),
            pltpu.VMEM(nodes, F32),
            pltpu.VMEM(nodes, F32),
            pltpu.VMEM(plane, BF),
            pltpu.VMEM(plane, BF),
            pltpu.VMEM((3,) + nodes, BF),
            pltpu.VMEM(plane, BF),
            pltpu.VMEM(plane, BF),
            pltpu.VMEM((256, 512), BF),
            pltpu.VMEM((256, 512), BF),
            pltpu.VMEM(nodes, BF),
            pltpu.VMEM(plane, BF),
            pltpu.VMEM(plane, BF),
            pltpu.VMEM((3,) + nodes, BF),
            pltpu.VMEM(plane, BF),
            pltpu.VMEM(plane, BF),
            pltpu.VMEM((256, 512), BF),
            pltpu.VMEM((256, 512), BF),
            pltpu.VMEM((512, 256), BF),
            pltpu.VMEM((512, 128), BF),
            pltpu.VMEM((512, 128), BF),
            pltpu.VMEM((512, 768), BF),
            pltpu.VMEM(nodes, BF),
            pltpu.VMEM(nodes, BF),
            pltpu.SemaphoreType.DMA((6,)),
            pltpu.SemaphoreType.DMA((2,)),
            pltpu.SemaphoreType.DMA((8,)),
            pltpu.SemaphoreType.DMA((8,)),
            pltpu.VMEM((2, 1536, 128), F32),
            pltpu.VMEM((2, 512, 128), F32),
            pltpu.VMEM((3, 512, 256), BF),
            pltpu.VMEM((3, 512, 256), BF),
            pltpu.VMEM((512, 256), BF),
            pltpu.VMEM((512, 256), BF),
            pltpu.SemaphoreType.DMA((4,)),
            pltpu.SemaphoreType.DMA((4,)),
        ] + scatter_scratch(),
        compiler_params=pltpu.CompilerParams(collective_id=0, has_side_effects=True, vmem_limit_bytes=64000000),
        name="mesh_step",
    )(node_features, edge_features, open_faces, edge_weight, node_weight, cotangent)
    return new_nodes, node_grad, edge_part.reshape(-1), node_part.reshape(-1)


def solution(mesh):
    placed = (
        P("gx", "gy", None, None),
        P(None, "gx", "gy", None, None),
        P(None, "gx", "gy", None),
        P(),
        P(),
        P("gx", "gy", None, None),
    )
    return jax.shard_map(
        local,
        mesh=mesh,
        in_specs=placed,
        out_specs=(
            P("gx", "gy", None, None),
            P("gx", "gy", None, None),
            P(("gx", "gy")),
            P(("gx", "gy")),
        ),
        check_vma=False,
    )
```

```python
import jax
import jax.numpy as jnp
from jax import lax
from jax.experimental import pallas as pl
from jax.experimental.pallas import tpu as pltpu
from jax.sharding import PartitionSpec as P

MESH = pl.DeviceIdType.MESH
BF = jnp.bfloat16
F32 = jnp.float32


class Place:
    def __init__(self):
        gx, gy = lax.axis_index("gx"), lax.axis_index("gy")
        self.gx, self.gy = gx, gy
        self.x_hi, self.y, self.core = gx // 16, (gx // 2) % 8, gx % 2
        self.z, self.x_lo = gy // 2, gy % 2
        self.x = self.x_hi * 2 + self.x_lo
        self.sibling = (gx + 1 - 2 * self.core, gy)

    def along(self, axis, step):
        if axis == "x":
            other = (self.x + step) % 4
            return other, ((other // 2) * 16 + self.y * 2 + self.core, self.z * 2 + other % 2)
        if axis == "y":
            other = (self.y + step) % 8
            return other, (self.x_hi * 16 + other * 2 + self.core, self.gy)
        other = (self.z + step) % 8
        return other, (self.gx, other * 2 + self.x_lo)

    def beside(self, first, second):
        return ((self.gx + first) % 32, (self.gy + second) % 16)

    def partners(self):
        found = [self.sibling, self.beside(1, 0), self.beside(-1, 0), self.beside(0, 1), self.beside(0, -1)]
        for axis, count in (("x", 4), ("y", 8), ("z", 8)):
            found += [self.along(axis, step)[1] for step in range(1, count)]
        return found


def greet(devices, meanwhile):
    barrier = pltpu.get_barrier_semaphore()
    for device in devices:
        pl.semaphore_signal(barrier, inc=1, device_id=device, device_id_type=MESH)
    meanwhile()
    pl.semaphore_wait(barrier, len(devices))


def push(source, target, send_sem, recv_sem, device):
    copy = pltpu.make_async_remote_copy(
        src_ref=source, dst_ref=target, send_sem=send_sem, recv_sem=recv_sem, device_id=device, device_id_type=MESH
    )
    copy.start()
    return copy


SIZES = {"x": 4, "y": 8, "z": 8}
FAR = {4: (2, 1, 3), 8: (4, 3, 5, 2, 6, 1, 7)}
ORDERS = (("x", "y", "z"), ("y", "x", "z"), ("z", "x", "y"), ("x", "z", "y"))
TYPES = {0: (0, 0), 1: (0, 1), 3: (1, 0), 2: (1, 1)}


def scatter_scratch():
    shapes = []
    for first, second, _ in ORDERS:
        one, two = SIZES[first], SIZES[second]
        shapes += [pltpu.VMEM((one, 2, two, 16, 128), BF)] * 2
        shapes += [pltpu.VMEM((two, 2, 16, 128), BF)] * 2
    shapes += [pltpu.VMEM((2, 64, 128), F32)]
    shapes += [pltpu.VMEM((2, 8, 8, 128), F32)] * 2
    shapes += [pltpu.VMEM((2, 8, 128), F32)] * 2
    shapes += [pltpu.SemaphoreType.DMA((4, 8))] * 4 + [pltpu.SemaphoreType.DMA((2, 8))] * 2
    shapes += [pltpu.SemaphoreType.DMA] * 2
    return shapes


def fill_first(place, plane, step, edge, node, out):
    first, second, _ = ORDERS[plane]
    dest, device = place.along(first, step)
    for c in range(2):
        if plane == 0:
            start = 768 * (dest // 2) + 3 * (dest % 2)
            rows = edge[c, pl.ds(start, 128, stride=6), :]
            out[step, c] = rows.astype(BF).reshape(8, 16, 128)
        elif plane == 1:
            for hi in range(2):
                for lo in range(2):
                    start = 768 * hi + 3 * lo + 1 + 96 * dest
                    out[step, c, 2 * hi + lo] = edge[c, pl.ds(start, 16, stride=6), :].astype(BF)
        elif plane == 2:
            for hi in range(2):
                for lo in range(2):
                    start = 768 * hi + 3 * lo + 2 + 6 * dest
                    rows = [edge[c, pl.ds(start + 48 * core, 8, stride=96), :] for core in range(2)]
                    out[step, c, 2 * hi + lo] = jnp.concatenate(rows, axis=0).astype(BF)
        else:
            for high in range(8):
                start = 256 * (dest // 2) + dest % 2 + 2 * high
                rows = [node[c, pl.ds(start + 16 * core, 8, stride=32), :] for core in range(2)]
                out[step, c, high] = jnp.concatenate(rows, axis=0).astype(BF)
    return device


def scatter(place, edge, node, scratch, meanwhile, planes_first=(1, 2, 0, 3)):
    bufs = [scratch[4 * plane: 4 * plane + 4] for plane in range(4)]
    wide, send_three, recv_three, last, last_in = scratch[16:21]
    send_1, recv_1, send_2, recv_2, send_3, recv_3, send_4, recv_4 = scratch[21:29]
    stage_1 = {plane: {} for plane in range(4)}
    stage_2 = {plane: {} for plane in range(4)}
    for plane in planes_first:
        first = ORDERS[plane][0]
        out, landing = bufs[plane][:2]
        for step in FAR[SIZES[first]]:
            device = fill_first(place, plane, step, edge, node, out)
            stage_1[plane][step] = push(out.at[step], landing.at[step], send_1.at[plane, step], recv_1.at[plane, step], device)
        fill_first(place, plane, 0, edge, node, out)
    meanwhile()
    for plane in planes_first:
        first, second, _ = ORDERS[plane]
        out, landing, out_2, landing_2 = bufs[plane]
        for step in (1, 7, 2, 6, 3, 5, 4) if SIZES[first] == 8 else (1, 3, 2):
            stage_1[plane][step].wait_recv()
        for step in FAR[SIZES[second]] + (0,):
            dest, device = place.along(second, step)
            total = out[0, :, dest].astype(F32)
            for source in range(1, SIZES[first]):
                total = total + landing[source, :, dest].astype(F32)
            out_2[step] = total.astype(BF)
            if step:
                stage_2[plane][step] = push(out_2.at[step], landing_2.at[step], send_2.at[plane, step], recv_2.at[plane, step], device)
    stage_3 = []
    for kind, axis in ((0, "z"), (1, "y")):
        for plane in range(4):
            if TYPES[plane][0] != kind:
                continue
            out_2, landing_2 = bufs[plane][2:]
            count = SIZES[ORDERS[plane][1]]
            for step in range(1, count):
                stage_2[plane][step].wait_recv()
            total = out_2[0].astype(F32)
            for source in range(1, count):
                total = total + landing_2[source].astype(F32)
            slot = TYPES[plane][1]
            for c in range(2):
                for core in range(2):
                    row = (core * 4 + slot * 2 + c) * 8
                    wide[kind, pl.ds(row, 8), :] = total[c, core * 8: core * 8 + 8]
        for step in FAR[8] + (0,):
            dest, device = place.along(axis, step)
            send_three[kind, step] = wide[kind, pl.ds(dest, 8, stride=8), :]
            if step:
                stage_3.append(push(send_three.at[kind, step], recv_three.at[kind, step], send_3.at[kind, step], recv_3.at[kind, step], device))
    for copy in stage_3:
        copy.wait_recv()
    for kind in range(2):
        total = send_three[kind, 0]
        for step in range(1, 8):
            total = total + recv_three[kind, step]
        last[kind] = total
    swap = push(last, last_in, send_4, recv_4, place.sibling)
    swap.wait_recv()
    pending = stage_3 + [swap]
    for plane in range(4):
        pending += list(stage_1[plane].values()) + list(stage_2[plane].values())

    def finish(edge_out, node_out):
        for plane in range(4):
            kind, slot = TYPES[plane]
            rows = pl.ds(place.core * 4 + slot * 2, 2)
            mine, theirs = last[kind, rows, :], last_in[kind, rows, :]
            low = jnp.where(place.core == 0, mine, theirs)
            high = jnp.where(place.core == 0, theirs, mine)
            if plane < 3:
                edge_out[pl.ds(4 * plane, 2), :] = low
                edge_out[pl.ds(4 * plane + 2, 2), :] = high
            else:
                node_out[pl.ds(0, 2), :] = low
                node_out[pl.ds(2, 2), :] = high
        for copy in pending:
            copy.wait_send()

    return finish


def mul(left, right):
    return jnp.dot(left, right, preferred_element_type=F32)


def mul_nt(left, right):
    return lax.dot_general(left, right, (((1,), (1,)), ((), ())), preferred_element_type=F32)


def mul_tn(left, right):
    return lax.dot_general(left, right, (((0,), (0,)), ((), ())), preferred_element_type=F32)


def sigmoid(value):
    return 0.5 + 0.5 * jnp.tanh(0.5 * value)


BLOCKS = ((0, 0), (0, 1), (1, 0), (1, 1))


def step_kernel(nf_in, ef_in, faces_in, we_in, wn_in, cot_in, nn_out, ng_out, edge_out, node_out,
                nf, ef, faces, we, wn, cot, spread, masks, pre, self_part, upper_part,
                halo, update, msg, in_x, in_y, summed, gu, gs, gs_x, gs_y, gp, gp_x, gp_y, gsum, tsum,
                nf_t, hx_t, hy_t, ef_t, nn, ng, load_sem, store_sem, halo_send, halo_recv,
                edge, node, edge_to, edge_from, node_to, node_from, swap_send, swap_recv, *scratch):
    place = Place()
    mine = pl.multiple_of(place.core * 256, 256)
    other = pl.multiple_of(256 - place.core * 256, 256)
    loads = []

    def load():
        for index, (source, target) in enumerate(((nf_in, nf), (we_in, we), (ef_in, ef), (faces_in, faces), (wn_in, wn), (cot_in, cot))):
            copy = pltpu.make_async_copy(source, target, load_sem.at[index])
            copy.start()
            loads.append(copy)

    greet(place.partners(), load)
    down_x, up_x = place.beside(-1, 0), place.beside(1, 0)
    down_y, up_y = place.beside(0, -1), place.beside(0, 1)
    halos = {}

    def trade(index, source, target, device):
        halos[index] = push(source, target, halo_send.at[index], halo_recv.at[index], device)

    for c in (1, 0):
        trade(2 + c, nf_in.at[pl.ds(128 * c, 64)], halo.at[c, 1], down_y)
        trade(c, nf_in.at[pl.ds(64 * c, 64)], halo.at[c, 0], down_x)

    loads[3].wait()
    spread[...] = jnp.zeros_like(spread)
    inside_x = jnp.where(place.gx < 31, 1.0, 0.0)
    inside_y = jnp.where(place.gy < 15, 1.0, 0.0)
    depth = lax.broadcasted_iota(jnp.int32, (2, 64), 1)
    second = lax.broadcasted_iota(jnp.int32, (2, 64), 0)
    for a in range(2):
        rows = faces[0, a].astype(F32)
        spread[pl.ds(2 * a, 2), :] = rows * inside_x if a else rows
        rows = faces[1, a].astype(F32)
        spread[pl.ds(4 + 2 * a, 2), :] = jnp.where(second == 1, rows * inside_y, rows)
        rows = faces[2, a].astype(F32)
        spread[pl.ds(8 + 2 * a, 2), :] = jnp.where(depth < 63, rows, 0.0)
    eye = lax.broadcasted_iota(jnp.int32, (64, 64), 0) == lax.broadcasted_iota(jnp.int32, (64, 64), 1)
    for row in range(12):
        column = jnp.where(eye, jnp.broadcast_to(spread[pl.ds(row, 1), :], (64, 64)), 0.0)
        masks[row] = jnp.broadcast_to(jnp.sum(column, axis=1, keepdims=True), (64, 128))

    loads[0].wait()
    loads[1].wait()
    own = nf[...]
    self_part[...] = mul(own, we[0:512, :]).reshape(2, 2, 64, 512)
    upper_part[...] = mul(own, we[512:1024, :]).reshape(2, 2, 64, 512)
    loads[2].wait()
    for d in (2, 1, 0):
        stored = mul(ef[d].reshape(256, 512), we[1024:1536, :]).reshape(2, 2, 64, 512)
        pre[d] = stored + self_part[...]

    def edge_block(d, a, b, upper):
        mask = jnp.concatenate([masks[4 * d + 2 * a + b]] * 4, axis=1)
        value = pre[d, a, b] + upper
        s = sigmoid(value)
        msg[d, a, b] = (value * s * mask).astype(BF)
        pre[d, a, b] = mask * (s * (1.0 + value * (1.0 - s)))

    @pl.loop(0, 2)
    def _(a):
        for b in range(2):
            edge_block(2, a, b, pltpu.roll(upper_part[a, b], 63, 0))
        edge_block(0, 0, a, upper_part[1, a])
        edge_block(1, a, 0, upper_part[a, 1])

    nf_t[...] = own.T

    for c in (1, 0):
        halos[2 + c].wait_recv()
        halos[c].wait_recv()
        self_part[c] = mul(halo[c].reshape(128, 512), we[512:1024, :]).reshape(2, 64, 512)

        @pl.loop(0, 2)
        def _(d):
            edge_block(d, 1 + d * (c - 1), c + d * (1 - c), self_part[c, d])

        trade(6 + c, msg.at[1, c, 1], in_y.at[c], up_y)
        trade(4 + c, msg.at[0, 1, c], in_x.at[c], up_x)

    for d in range(3):
        ef_t[:, 256 * d: 256 * d + 256] = ef[d].reshape(256, 512).T
    hx_t[...] = jnp.concatenate([halo[0, 0], halo[1, 0]], axis=0).T
    hy_t[...] = jnp.concatenate([halo[0, 1], halo[1, 1]], axis=0).T
    loads[4].wait()
    loads[5].wait()

    def node_blocks(blocks):
        for a, b in blocks:
            third = msg[2, a, b].astype(F32)
            total = msg[0, a, b].astype(F32) + msg[1, a, b].astype(F32) + third
            total = total - pltpu.roll(third, 1, 0)
            total = total - (in_x[b] if a == 0 else msg[0, 0, b]).astype(F32)
            total = total - (in_y[a] if b == 0 else msg[1, a, 0]).astype(F32)
            summed[pl.ds(128 * a + 64 * b, 64), :] = total.astype(BF)

    def node_update(low, high):
        rows = pl.ds(64 * low, 64 * (high - low))
        update[rows, :] = mul(summed[rows, :], wn[...])

        @pl.loop(2 * low, 2 * high)
        def _(half):
            part = pl.ds(pl.multiple_of(32 * half, 32), 32)
            value = update[part, :]
            s = sigmoid(value)
            nn[part, :] = (nf[part, :].astype(F32) + value * s).astype(BF)
            gu[part, :] = (cot[part, :].astype(F32) * (s * (1.0 + value * (1.0 - s)))).astype(BF)

        gs[rows, :] = mul_nt(gu[rows, :], wn[...]).astype(BF)

    halos[7].wait_recv()
    halos[5].wait_recv()
    node_blocks(((0, 1), (1, 0), (1, 1)))
    node_update(1, 4)
    trade(11, gs.at[pl.ds(128, 64)], gs_y.at[1], down_y)
    trade(9, gs.at[pl.ds(64, 64)], gs_x.at[1], down_x)
    halos[6].wait_recv()
    halos[4].wait_recv()
    node_blocks(((0, 0),))
    node_update(0, 1)
    trade(10, gs.at[pl.ds(0, 64)], gs_y.at[0], down_y)
    trade(8, gs.at[pl.ds(0, 64)], gs_x.at[0], down_x)
    store_nn = pltpu.make_async_copy(nn, nn_out, store_sem.at[0])
    store_nn.start()

    node_to[...] = mul_tn(summed[...], gu[:, pl.ds(other, 256)]).astype(BF)
    swaps = [push(node_to, node_from, swap_send.at[3], swap_recv.at[3], place.sibling)]
    for c in range(2):
        node[c] = mul_tn(summed[...], gu[:, pl.ds(pl.multiple_of(mine + 128 * c, 128), 128)])

    def gs_block(a, b):
        return gs[pl.ds(128 * a + 64 * b, 64), :].astype(F32)

    def grad_block(d, a, b, above):
        gp[d, a, b] = ((gs_block(a, b) - above) * pre[d, a, b]).astype(BF)

    for a, b in BLOCKS:
        grad_block(2, a, b, pltpu.roll(gs_block(a, b), 63, 0))
    for b in range(2):
        grad_block(0, 0, b, gs_block(1, b))
    for a in range(2):
        grad_block(1, a, 0, gs_block(a, 1))
    swaps[0].wait_recv()
    for c in range(2):
        node[c] = node[c] + node_from[:, 128 * c: 128 * c + 128].astype(F32)
    halos[11].wait_recv()
    halos[10].wait_recv()
    for a in range(2):
        grad_block(1, a, 1, gs_y[a].astype(F32))
    trade(13, gp.at[1, :, 1], gp_y, up_y)
    halos[9].wait_recv()
    halos[8].wait_recv()
    for b in range(2):
        grad_block(0, 1, b, gs_x[b].astype(F32))
    trade(12, gp.at[0, 1], gp_x, up_x)
    for a, b in BLOCKS:
        rows = pl.ds(128 * a + 64 * b, 64)
        third = gp[2, a, b].astype(F32)
        gsum[rows, :] = (gp[0, a, b].astype(F32) + gp[1, a, b].astype(F32) + third).astype(BF)
        total = pltpu.roll(third, 1, 0)
        if a:
            total = total + gp[0, 0, b].astype(F32)
        if b:
            total = total + gp[1, a, 0].astype(F32)
        tsum[rows, :] = total.astype(BF)

    def grads(part, columns):
        if part == 0:
            return mul(nf_t[...], gsum[:, columns])
        if part == 1:
            total = mul(nf_t[...], tsum[:, columns])
            total = total + mul(hx_t[...], gp[0, 1, :, :, columns].reshape(128, 256))
            return total + mul(hy_t[...], gp[1, :, 1, :, columns].reshape(128, 256))
        return mul(ef_t[...], gp[:, :, :, :, columns].reshape(768, 256))

    for part in range(3):
        edge_to[part] = grads(part, pl.ds(other, 256)).astype(BF)
        swaps.append(push(edge_to.at[part], edge_from.at[part], swap_send.at[part], swap_recv.at[part], place.sibling))
    for part in range(3):
        total = grads(part, pl.ds(mine, 256))
        for c in range(2):
            edge[c, pl.ds(512 * part, 512), :] = total[:, 128 * c: 128 * c + 128]
    for part in range(3):
        swaps[part + 1].wait_recv()
        for c in range(2):
            rows = pl.ds(512 * part, 512)
            edge[c, rows, :] = edge[c, rows, :] + edge_from[part, :, 128 * c: 128 * c + 128].astype(F32)

    def node_grads():
        halos[12].wait_recv()
        halos[13].wait_recv()
        for a, b in BLOCKS:
            total = pltpu.roll(gp[2, a, b].astype(F32), 1, 0)
            total = total + (gp[0, 0, b] if a else gp_x[b]).astype(F32)
            total = total + (gp[1, a, 0] if b else gp_y[a]).astype(F32)
            tsum[pl.ds(128 * a + 64 * b, 64), :] = total.astype(BF)
        upper_part[...] = (mul_nt(gsum[...], we[0:512, :]) + mul_nt(tsum[...], we[512:1024, :])).reshape(2, 2, 64, 512)

        @pl.loop(0, 4)
        def _(block):
            a, b = block // 2, block % 2
            part = pl.ds(pl.multiple_of(64 * block, 64), 64)
            ng[part, :] = (cot[part, :].astype(F32) + upper_part[a, b]).astype(BF)

        pltpu.make_async_copy(ng, ng_out, store_sem.at[1]).start()

    finish = scatter(place, edge, node, scratch, node_grads)
    finish(edge_out, node_out)
    for copy in swaps + list(halos.values()):
        copy.wait_send()
    store_nn.wait()
    pltpu.make_async_copy(ng, ng_out, store_sem.at[1]).wait()


def settle_kernel(*refs):
    copies = [pltpu.make_async_copy(refs[i], refs[4 + i], refs[8].at[i]) for i in range(4)]
    for copy in copies:
        copy.start()
    for copy in copies:
        copy.wait()


def local(node_features, edge_features, open_faces, edge_weight, node_weight, cotangent):
    anywhere = pl.BlockSpec(memory_space=pltpu.HBM)
    vmem = pl.BlockSpec(memory_space=pltpu.VMEM)
    nodes, flat = (2, 2, 64, 512), (256, 512)
    plane = (2, 64, 512)
    new_nodes, node_grad, edge_part, node_part = pl.pallas_call(
        step_kernel,
        out_shape=(
            jax.ShapeDtypeStruct(flat, BF),
            jax.ShapeDtypeStruct(flat, BF),
            jax.ShapeDtypeStruct((12, 128), F32),
            jax.ShapeDtypeStruct((4, 128), F32),
        ),
        in_specs=[anywhere] * 6,
        out_specs=(anywhere, anywhere, vmem, vmem),
        scratch_shapes=[
            pltpu.VMEM(flat, BF),
            pltpu.VMEM((3,) + nodes, BF),
            pltpu.VMEM((3, 2, 2, 64), jnp.int32),
            pltpu.VMEM((1536, 512), BF),
            pltpu.VMEM((512, 512), BF),
            pltpu.VMEM(flat, BF),
            pltpu.VMEM((16, 64), F32),
            pltpu.VMEM((12, 64, 128), F32),
            pltpu.VMEM((3,) + nodes, F32),
            pltpu.VMEM(nodes, F32),
            pltpu.VMEM(nodes, F32),
            pltpu.VMEM(nodes, BF),
            pltpu.VMEM(flat, F32),
            pltpu.VMEM((3,) + nodes, BF),
            pltpu.VMEM(plane, BF),
            pltpu.VMEM(plane, BF),
            pltpu.VMEM((256, 512), BF),
            pltpu.VMEM((256, 512), BF),
            pltpu.VMEM(flat, BF),
            pltpu.VMEM(plane, BF),
            pltpu.VMEM(plane, BF),
            pltpu.VMEM((3,) + nodes, BF),
            pltpu.VMEM(plane, BF),
            pltpu.VMEM(plane, BF),
            pltpu.VMEM((256, 512), BF),
            pltpu.VMEM((256, 512), BF),
            pltpu.VMEM((512, 256), BF),
            pltpu.VMEM((512, 128), BF),
            pltpu.VMEM((512, 128), BF),
            pltpu.VMEM((512, 768), BF),
            pltpu.VMEM(flat, BF),
            pltpu.VMEM(flat, BF),
            pltpu.SemaphoreType.DMA((6,)),
            pltpu.SemaphoreType.DMA((2,)),
            pltpu.SemaphoreType.DMA((14,)),
            pltpu.SemaphoreType.DMA((14,)),
            pltpu.VMEM((2, 1536, 128), F32),
            pltpu.VMEM((2, 512, 128), F32),
            pltpu.VMEM((3, 512, 256), BF),
            pltpu.VMEM((3, 512, 256), BF),
            pltpu.VMEM((512, 256), BF),
            pltpu.VMEM((512, 256), BF),
            pltpu.SemaphoreType.DMA((4,)),
            pltpu.SemaphoreType.DMA((4,)),
        ] + scatter_scratch(),
        compiler_params=pltpu.CompilerParams(collective_id=0, has_side_effects=True, vmem_limit_bytes=64000000),
        name="mesh_step",
    )(node_features.reshape(flat), edge_features, open_faces, edge_weight, node_weight, cotangent.reshape(flat))
    new_nodes, node_grad, edge_part, node_part = pl.pallas_call(
        settle_kernel,
        out_shape=(
            jax.ShapeDtypeStruct(flat, BF),
            jax.ShapeDtypeStruct(flat, BF),
            jax.ShapeDtypeStruct((12, 128), F32),
            jax.ShapeDtypeStruct((4, 128), F32),
        ),
        in_specs=[pl.BlockSpec(memory_space=pl.ANY)] * 4,
        out_specs=(vmem,) * 4,
        scratch_shapes=[pltpu.SemaphoreType.DMA((4,))],
        compiler_params=pltpu.CompilerParams(vmem_limit_bytes=4 * 1024 * 1024),
        name="settle",
    )(new_nodes, node_grad, edge_part, node_part)
    return new_nodes.reshape(nodes), node_grad.reshape(nodes), edge_part.reshape(-1), node_part.reshape(-1)


def solution(mesh):
    placed = (
        P("gx", "gy", None, None),
        P(None, "gx", "gy", None, None),
        P(None, "gx", "gy", None),
        P(),
        P(),
        P("gx", "gy", None, None),
    )
    return jax.shard_map(
        local,
        mesh=mesh,
        in_specs=placed,
        out_specs=(
            P("gx", "gy", None, None),
            P("gx", "gy", None, None),
            P(("gx", "gy")),
            P(("gx", "gy")),
        ),
        check_vma=False,
    )
```

```python
import jax
import jax.numpy as jnp
from jax import lax
from jax.experimental import pallas as pl
from jax.experimental.pallas import tpu as pltpu
from jax.sharding import PartitionSpec as P

MESH = pl.DeviceIdType.MESH
BF = jnp.bfloat16
F32 = jnp.float32


class Place:
    def __init__(self):
        gx, gy = lax.axis_index("gx"), lax.axis_index("gy")
        self.gx, self.gy = gx, gy
        self.x_hi, self.y, self.core = gx // 16, (gx // 2) % 8, gx % 2
        self.z, self.x_lo = gy // 2, gy % 2
        self.x = self.x_hi * 2 + self.x_lo
        self.sibling = (gx + 1 - 2 * self.core, gy)

    def along(self, axis, step):
        if axis == "x":
            other = (self.x + step) % 4
            return other, ((other // 2) * 16 + self.y * 2 + self.core, self.z * 2 + other % 2)
        if axis == "y":
            other = (self.y + step) % 8
            return other, (self.x_hi * 16 + other * 2 + self.core, self.gy)
        other = (self.z + step) % 8
        return other, (self.gx, other * 2 + self.x_lo)

    def beside(self, first, second):
        return ((self.gx + first) % 32, (self.gy + second) % 16)

    def partners(self):
        found = [self.sibling, self.beside(1, 0), self.beside(-1, 0), self.beside(0, 1), self.beside(0, -1)]
        for axis, count in (("x", 4), ("y", 8), ("z", 8)):
            found += [self.along(axis, step)[1] for step in range(1, count)]
        return found


def greet(devices, meanwhile):
    barrier = pltpu.get_barrier_semaphore()
    for device in devices:
        pl.semaphore_signal(barrier, inc=1, device_id=device, device_id_type=MESH)
    meanwhile()
    pl.semaphore_wait(barrier, len(devices))


def push(source, target, send_sem, recv_sem, device):
    copy = pltpu.make_async_remote_copy(
        src_ref=source, dst_ref=target, send_sem=send_sem, recv_sem=recv_sem, device_id=device, device_id_type=MESH
    )
    copy.start()
    return copy


SIZES = {"x": 4, "y": 8, "z": 8}
FAR = {4: (2, 1, 3), 8: (4, 3, 5, 2, 6, 1, 7)}
ORDERS = (("x", "y", "z"), ("y", "x", "z"), ("z", "x", "y"), ("x", "z", "y"))
TYPES = {0: (0, 0), 1: (0, 1), 3: (1, 0), 2: (1, 1)}


def scatter_scratch():
    shapes = []
    for first, second, _ in ORDERS:
        one, two = SIZES[first], SIZES[second]
        shapes += [pltpu.VMEM((one, 2, two, 16, 128), BF)] * 2
        shapes += [pltpu.VMEM((two, 2, 16, 128), BF)] * 2
    shapes += [pltpu.VMEM((2, 64, 128), F32)]
    shapes += [pltpu.VMEM((2, 8, 8, 128), F32)] * 2
    shapes += [pltpu.VMEM((2, 8, 128), F32)] * 2
    shapes += [pltpu.SemaphoreType.DMA((4, 8))] * 4 + [pltpu.SemaphoreType.DMA((2, 8))] * 2
    shapes += [pltpu.SemaphoreType.DMA] * 2
    return shapes


def fill_first(place, plane, step, edge, node, out):
    first, second, _ = ORDERS[plane]
    dest, device = place.along(first, step)
    for c in range(2):
        if plane == 0:
            start = 768 * (dest // 2) + 3 * (dest % 2)
            rows = edge[c, pl.ds(start, 128, stride=6), :]
            out[step, c] = rows.astype(BF).reshape(8, 16, 128)
        elif plane == 1:
            for hi in range(2):
                for lo in range(2):
                    start = 768 * hi + 3 * lo + 1 + 96 * dest
                    out[step, c, 2 * hi + lo] = edge[c, pl.ds(start, 16, stride=6), :].astype(BF)
        elif plane == 2:
            for hi in range(2):
                for lo in range(2):
                    start = 768 * hi + 3 * lo + 2 + 6 * dest
                    rows = [edge[c, pl.ds(start + 48 * core, 8, stride=96), :] for core in range(2)]
                    out[step, c, 2 * hi + lo] = jnp.concatenate(rows, axis=0).astype(BF)
        else:
            for high in range(8):
                start = 256 * (dest // 2) + dest % 2 + 2 * high
                rows = [node[c, pl.ds(start + 16 * core, 8, stride=32), :] for core in range(2)]
                out[step, c, high] = jnp.concatenate(rows, axis=0).astype(BF)
    return device


def scatter(place, edge, node, scratch, meanwhile, planes_first=(1, 2, 0, 3)):
    bufs = [scratch[4 * plane: 4 * plane + 4] for plane in range(4)]
    wide, send_three, recv_three, last, last_in = scratch[16:21]
    send_1, recv_1, send_2, recv_2, send_3, recv_3, send_4, recv_4 = scratch[21:29]
    stage_1 = {plane: {} for plane in range(4)}
    stage_2 = {plane: {} for plane in range(4)}
    for plane in planes_first:
        first = ORDERS[plane][0]
        out, landing = bufs[plane][:2]
        for step in FAR[SIZES[first]]:
            device = fill_first(place, plane, step, edge, node, out)
            stage_1[plane][step] = push(out.at[step], landing.at[step], send_1.at[plane, step], recv_1.at[plane, step], device)
        fill_first(place, plane, 0, edge, node, out)
    meanwhile()
    for plane in planes_first:
        first, second, _ = ORDERS[plane]
        out, landing, out_2, landing_2 = bufs[plane]
        for step in (1, 7, 2, 6, 3, 5, 4) if SIZES[first] == 8 else (1, 3, 2):
            stage_1[plane][step].wait_recv()
        for step in FAR[SIZES[second]] + (0,):
            dest, device = place.along(second, step)
            total = out[0, :, dest].astype(F32)
            for source in range(1, SIZES[first]):
                total = total + landing[source, :, dest].astype(F32)
            out_2[step] = total.astype(BF)
            if step:
                stage_2[plane][step] = push(out_2.at[step], landing_2.at[step], send_2.at[plane, step], recv_2.at[plane, step], device)
    stage_3 = []
    for kind, axis in ((0, "z"), (1, "y")):
        for plane in range(4):
            if TYPES[plane][0] != kind:
                continue
            out_2, landing_2 = bufs[plane][2:]
            count = SIZES[ORDERS[plane][1]]
            for step in range(1, count):
                stage_2[plane][step].wait_recv()
            total = out_2[0].astype(F32)
            for source in range(1, count):
                total = total + landing_2[source].astype(F32)
            slot = TYPES[plane][1]
            for c in range(2):
                for core in range(2):
                    row = (core * 4 + slot * 2 + c) * 8
                    wide[kind, pl.ds(row, 8), :] = total[c, core * 8: core * 8 + 8]
        for step in FAR[8] + (0,):
            dest, device = place.along(axis, step)
            send_three[kind, step] = wide[kind, pl.ds(dest, 8, stride=8), :]
            if step:
                stage_3.append(push(send_three.at[kind, step], recv_three.at[kind, step], send_3.at[kind, step], recv_3.at[kind, step], device))
    for copy in stage_3:
        copy.wait_recv()
    for kind in range(2):
        total = send_three[kind, 0]
        for step in range(1, 8):
            total = total + recv_three[kind, step]
        last[kind] = total
    swap = push(last, last_in, send_4, recv_4, place.sibling)
    swap.wait_recv()
    pending = stage_3 + [swap]
    for plane in range(4):
        pending += list(stage_1[plane].values()) + list(stage_2[plane].values())

    def finish(edge_out, node_out):
        for plane in range(4):
            kind, slot = TYPES[plane]
            rows = pl.ds(place.core * 4 + slot * 2, 2)
            mine, theirs = last[kind, rows, :], last_in[kind, rows, :]
            low = jnp.where(place.core == 0, mine, theirs)
            high = jnp.where(place.core == 0, theirs, mine)
            if plane < 3:
                edge_out[pl.ds(4 * plane, 2), :] = low
                edge_out[pl.ds(4 * plane + 2, 2), :] = high
            else:
                node_out[pl.ds(0, 2), :] = low
                node_out[pl.ds(2, 2), :] = high
        for copy in pending:
            copy.wait_send()

    return finish


def mul(left, right):
    return jnp.dot(left, right, preferred_element_type=F32)


def mul_nt(left, right):
    return lax.dot_general(left, right, (((1,), (1,)), ((), ())), preferred_element_type=F32)


def mul_tn(left, right):
    return lax.dot_general(left, right, (((0,), (0,)), ((), ())), preferred_element_type=F32)


def sigmoid(value):
    return 0.5 + 0.5 * jnp.tanh(0.5 * value)


BLOCKS = ((0, 0), (0, 1), (1, 0), (1, 1))


def step_kernel(nf_in, ef_in, faces_in, we_in, wn_in, cot_in, nn_out, ng_out, edge_out, node_out,
                nf, ef, faces, we, wn, cot, spread, masks, pre, self_part, upper_part,
                halo, update, msg, in_x, in_y, summed, gu, gs, gs_x, gs_y, gp, gp_x, gp_y, gsum, tsum,
                nf_t, hx_t, hy_t, ef_t, nn, ng, load_sem, store_sem, halo_send, halo_recv,
                edge, node, edge_to, edge_from, node_to, node_from, swap_send, swap_recv, *scratch):
    place = Place()
    mine = pl.multiple_of(place.core * 256, 256)
    other = pl.multiple_of(256 - place.core * 256, 256)
    loads = []

    def load():
        for index, (source, target) in enumerate(((nf_in, nf), (we_in, we), (ef_in, ef), (faces_in, faces), (wn_in, wn), (cot_in, cot))):
            copy = pltpu.make_async_copy(source, target, load_sem.at[index])
            copy.start()
            loads.append(copy)

    greet(place.partners(), load)
    down_x, up_x = place.beside(-1, 0), place.beside(1, 0)
    down_y, up_y = place.beside(0, -1), place.beside(0, 1)
    halos = {}

    def trade(index, source, target, device):
        halos[index] = push(source, target, halo_send.at[index], halo_recv.at[index], device)

    for c in (1, 0):
        trade(2 + c, nf_in.at[pl.ds(128 * c, 64)], halo.at[c, 1], down_y)
        trade(c, nf_in.at[pl.ds(64 * c, 64)], halo.at[c, 0], down_x)

    loads[3].wait()
    spread[...] = jnp.zeros_like(spread)
    inside_x = jnp.where(place.gx < 31, 1.0, 0.0)
    inside_y = jnp.where(place.gy < 15, 1.0, 0.0)
    depth = lax.broadcasted_iota(jnp.int32, (2, 64), 1)
    second = lax.broadcasted_iota(jnp.int32, (2, 64), 0)
    for a in range(2):
        rows = faces[0, a].astype(F32)
        spread[pl.ds(2 * a, 2), :] = rows * inside_x if a else rows
        rows = faces[1, a].astype(F32)
        spread[pl.ds(4 + 2 * a, 2), :] = jnp.where(second == 1, rows * inside_y, rows)
        rows = faces[2, a].astype(F32)
        spread[pl.ds(8 + 2 * a, 2), :] = jnp.where(depth < 63, rows, 0.0)
    eye = lax.broadcasted_iota(jnp.int32, (64, 64), 0) == lax.broadcasted_iota(jnp.int32, (64, 64), 1)
    for row in range(12):
        column = jnp.where(eye, jnp.broadcast_to(spread[pl.ds(row, 1), :], (64, 64)), 0.0)
        masks[row] = jnp.broadcast_to(jnp.sum(column, axis=1, keepdims=True), (64, 128))

    loads[0].wait()
    loads[1].wait()
    own = nf[...]
    self_part[...] = mul(own, we[0:512, :]).reshape(2, 2, 64, 512)
    upper_part[...] = mul(own, we[512:1024, :]).reshape(2, 2, 64, 512)
    loads[2].wait()
    for d in (2, 1, 0):
        stored = mul(ef[d].reshape(256, 512), we[1024:1536, :]).reshape(2, 2, 64, 512)
        pre[d] = stored + self_part[...]

    def edge_block(d, a, b, upper):
        mask = jnp.concatenate([masks[4 * d + 2 * a + b]] * 4, axis=1)
        value = pre[d, a, b] + upper
        s = sigmoid(value)
        msg[d, a, b] = (value * s * mask).astype(BF)
        pre[d, a, b] = mask * (s * (1.0 + value * (1.0 - s)))

    @pl.loop(0, 2)
    def _(a):
        for b in range(2):
            edge_block(2, a, b, pltpu.roll(upper_part[a, b], 63, 0))
        edge_block(0, 0, a, upper_part[1, a])
        edge_block(1, a, 0, upper_part[a, 1])

    nf_t[...] = own.T

    for c in (1, 0):
        halos[2 + c].wait_recv()
        halos[c].wait_recv()
        self_part[c] = mul(halo[c].reshape(128, 512), we[512:1024, :]).reshape(2, 64, 512)

        @pl.loop(0, 2)
        def _(d):
            edge_block(d, 1 + d * (c - 1), c + d * (1 - c), self_part[c, d])

        trade(6 + c, msg.at[1, c, 1], in_y.at[c], up_y)
        trade(4 + c, msg.at[0, 1, c], in_x.at[c], up_x)

    for d in range(3):
        ef_t[:, 256 * d: 256 * d + 256] = ef[d].reshape(256, 512).T
    hx_t[...] = jnp.concatenate([halo[0, 0], halo[1, 0]], axis=0).T
    hy_t[...] = jnp.concatenate([halo[0, 1], halo[1, 1]], axis=0).T
    loads[4].wait()
    loads[5].wait()

    def node_blocks(blocks):
        for a, b in blocks:
            third = msg[2, a, b].astype(F32)
            total = msg[0, a, b].astype(F32) + msg[1, a, b].astype(F32) + third
            total = total - pltpu.roll(third, 1, 0)
            total = total - (in_x[b] if a == 0 else msg[0, 0, b]).astype(F32)
            total = total - (in_y[a] if b == 0 else msg[1, a, 0]).astype(F32)
            summed[pl.ds(128 * a + 64 * b, 64), :] = total.astype(BF)

    def node_update(low, high):
        rows = pl.ds(64 * low, 64 * (high - low))
        update[rows, :] = mul(summed[rows, :], wn[...])

        @pl.loop(2 * low, 2 * high)
        def _(half):
            part = pl.ds(pl.multiple_of(32 * half, 32), 32)
            value = update[part, :]
            s = sigmoid(value)
            nn[part, :] = (nf[part, :].astype(F32) + value * s).astype(BF)
            gu[part, :] = (cot[part, :].astype(F32) * (s * (1.0 + value * (1.0 - s)))).astype(BF)

        gs[rows, :] = mul_nt(gu[rows, :], wn[...]).astype(BF)

    halos[7].wait_recv()
    halos[5].wait_recv()
    node_blocks(((0, 1), (1, 0), (1, 1)))
    node_update(1, 4)
    trade(11, gs.at[pl.ds(128, 64)], gs_y.at[1], down_y)
    trade(9, gs.at[pl.ds(64, 64)], gs_x.at[1], down_x)
    halos[6].wait_recv()
    halos[4].wait_recv()
    node_blocks(((0, 0),))
    node_update(0, 1)
    trade(10, gs.at[pl.ds(0, 64)], gs_y.at[0], down_y)
    trade(8, gs.at[pl.ds(0, 64)], gs_x.at[0], down_x)
    store_nn = pltpu.make_async_copy(nn, nn_out, store_sem.at[0])
    store_nn.start()

    node_to[...] = mul_tn(summed[...], gu[:, pl.ds(other, 256)]).astype(BF)
    swaps = [push(node_to, node_from, swap_send.at[3], swap_recv.at[3], place.sibling)]
    for c in range(2):
        node[c] = mul_tn(summed[...], gu[:, pl.ds(pl.multiple_of(mine + 128 * c, 128), 128)])

    def gs_block(a, b):
        return gs[pl.ds(128 * a + 64 * b, 64), :].astype(F32)

    def grad_block(d, a, b, above):
        gp[d, a, b] = ((gs_block(a, b) - above) * pre[d, a, b]).astype(BF)

    for a, b in BLOCKS:
        grad_block(2, a, b, pltpu.roll(gs_block(a, b), 63, 0))
    for b in range(2):
        grad_block(0, 0, b, gs_block(1, b))
    for a in range(2):
        grad_block(1, a, 0, gs_block(a, 1))
    swaps[0].wait_recv()
    for c in range(2):
        node[c] = node[c] + node_from[:, 128 * c: 128 * c + 128].astype(F32)
    halos[11].wait_recv()
    halos[10].wait_recv()
    for a in range(2):
        grad_block(1, a, 1, gs_y[a].astype(F32))
    trade(13, gp.at[1, :, 1], gp_y, up_y)
    halos[9].wait_recv()
    halos[8].wait_recv()
    for b in range(2):
        grad_block(0, 1, b, gs_x[b].astype(F32))
    trade(12, gp.at[0, 1], gp_x, up_x)
    for a, b in BLOCKS:
        rows = pl.ds(128 * a + 64 * b, 64)
        third = gp[2, a, b].astype(F32)
        gsum[rows, :] = (gp[0, a, b].astype(F32) + gp[1, a, b].astype(F32) + third).astype(BF)
        total = pltpu.roll(third, 1, 0)
        if a:
            total = total + gp[0, 0, b].astype(F32)
        if b:
            total = total + gp[1, a, 0].astype(F32)
        tsum[rows, :] = total.astype(BF)

    def grads(part, columns):
        if part == 0:
            return mul(nf_t[...], gsum[:, columns])
        if part == 1:
            total = mul(nf_t[...], tsum[:, columns])
            total = total + mul(hx_t[...], gp[0, 1, :, :, columns].reshape(128, 256))
            return total + mul(hy_t[...], gp[1, :, 1, :, columns].reshape(128, 256))
        return mul(ef_t[...], gp[:, :, :, :, columns].reshape(768, 256))

    for part in range(3):
        edge_to[part] = grads(part, pl.ds(other, 256)).astype(BF)
        swaps.append(push(edge_to.at[part], edge_from.at[part], swap_send.at[part], swap_recv.at[part], place.sibling))
    for part in range(3):
        total = grads(part, pl.ds(mine, 256))
        for c in range(2):
            edge[c, pl.ds(512 * part, 512), :] = total[:, 128 * c: 128 * c + 128]
    for part in range(3):
        swaps[part + 1].wait_recv()
        for c in range(2):
            rows = pl.ds(512 * part, 512)
            edge[c, rows, :] = edge[c, rows, :] + edge_from[part, :, 128 * c: 128 * c + 128].astype(F32)

    def node_grads():
        halos[12].wait_recv()
        halos[13].wait_recv()
        for a, b in BLOCKS:
            total = pltpu.roll(gp[2, a, b].astype(F32), 1, 0)
            total = total + (gp[0, 0, b] if a else gp_x[b]).astype(F32)
            total = total + (gp[1, a, 0] if b else gp_y[a]).astype(F32)
            tsum[pl.ds(128 * a + 64 * b, 64), :] = total.astype(BF)
        upper_part[...] = (mul_nt(gsum[...], we[0:512, :]) + mul_nt(tsum[...], we[512:1024, :])).reshape(2, 2, 64, 512)

        @pl.loop(0, 4)
        def _(block):
            a, b = block // 2, block % 2
            part = pl.ds(pl.multiple_of(64 * block, 64), 64)
            ng[part, :] = (cot[part, :].astype(F32) + upper_part[a, b]).astype(BF)

        pltpu.make_async_copy(ng, ng_out, store_sem.at[1]).start()

    finish = scatter(place, edge, node, scratch, node_grads)
    finish(edge_out, node_out)
    for copy in swaps + list(halos.values()):
        copy.wait_send()
    store_nn.wait()
    pltpu.make_async_copy(ng, ng_out, store_sem.at[1]).wait()


def settle_kernel(*refs):
    copies = [pltpu.make_async_copy(refs[i], refs[4 + i], refs[8].at[i]) for i in range(4)]
    for copy in copies:
        copy.start()
    for copy in copies:
        copy.wait()


def local(node_features, edge_features, open_faces, edge_weight, node_weight, cotangent):
    anywhere = pl.BlockSpec(memory_space=pltpu.HBM)
    vmem = pl.BlockSpec(memory_space=pltpu.VMEM)
    nodes, flat = (2, 2, 64, 512), (256, 512)
    plane = (2, 64, 512)
    new_nodes, node_grad, edge_part, node_part = pl.pallas_call(
        step_kernel,
        out_shape=(
            jax.ShapeDtypeStruct(flat, BF),
            jax.ShapeDtypeStruct(flat, BF),
            jax.ShapeDtypeStruct((12, 128), F32),
            jax.ShapeDtypeStruct((4, 128), F32),
        ),
        in_specs=[anywhere] * 6,
        out_specs=(anywhere, anywhere, vmem, vmem),
        scratch_shapes=[
            pltpu.VMEM(flat, BF),
            pltpu.VMEM((3,) + nodes, BF),
            pltpu.VMEM((3, 2, 2, 64), jnp.int32),
            pltpu.VMEM((1536, 512), BF),
            pltpu.VMEM((512, 512), BF),
            pltpu.VMEM(flat, BF),
            pltpu.VMEM((16, 64), F32),
            pltpu.VMEM((12, 64, 128), F32),
            pltpu.VMEM((3,) + nodes, F32),
            pltpu.VMEM(nodes, F32),
            pltpu.VMEM(nodes, F32),
            pltpu.VMEM(nodes, BF),
            pltpu.VMEM(flat, F32),
            pltpu.VMEM((3,) + nodes, BF),
            pltpu.VMEM(plane, BF),
            pltpu.VMEM(plane, BF),
            pltpu.VMEM((256, 512), BF),
            pltpu.VMEM((256, 512), BF),
            pltpu.VMEM(flat, BF),
            pltpu.VMEM(plane, BF),
            pltpu.VMEM(plane, BF),
            pltpu.VMEM((3,) + nodes, BF),
            pltpu.VMEM(plane, BF),
            pltpu.VMEM(plane, BF),
            pltpu.VMEM((256, 512), BF),
            pltpu.VMEM((256, 512), BF),
            pltpu.VMEM((512, 256), BF),
            pltpu.VMEM((512, 128), BF),
            pltpu.VMEM((512, 128), BF),
            pltpu.VMEM((512, 768), BF),
            pltpu.VMEM(flat, BF),
            pltpu.VMEM(flat, BF),
            pltpu.SemaphoreType.DMA((6,)),
            pltpu.SemaphoreType.DMA((2,)),
            pltpu.SemaphoreType.DMA((14,)),
            pltpu.SemaphoreType.DMA((14,)),
            pltpu.VMEM((2, 1536, 128), F32),
            pltpu.VMEM((2, 512, 128), F32),
            pltpu.VMEM((3, 512, 256), BF),
            pltpu.VMEM((3, 512, 256), BF),
            pltpu.VMEM((512, 256), BF),
            pltpu.VMEM((512, 256), BF),
            pltpu.SemaphoreType.DMA((4,)),
            pltpu.SemaphoreType.DMA((4,)),
        ] + scatter_scratch(),
        compiler_params=pltpu.CompilerParams(collective_id=0, has_side_effects=True, vmem_limit_bytes=64000000),
        name="mesh_step",
    )(node_features.reshape(flat), edge_features, open_faces, edge_weight, node_weight, cotangent.reshape(flat))
    new_nodes, node_grad, edge_part, node_part = pl.pallas_call(
        settle_kernel,
        out_shape=(
            jax.ShapeDtypeStruct(flat, BF),
            jax.ShapeDtypeStruct(flat, BF),
            jax.ShapeDtypeStruct((12, 128), F32),
            jax.ShapeDtypeStruct((4, 128), F32),
        ),
        in_specs=[pl.BlockSpec(memory_space=pl.ANY)] * 4,
        out_specs=(vmem,) * 4,
        scratch_shapes=[pltpu.SemaphoreType.DMA((4,))],
        compiler_params=pltpu.CompilerParams(vmem_limit_bytes=64000000),
        name="settle",
    )(new_nodes, node_grad, edge_part, node_part)
    return new_nodes.reshape(nodes), node_grad.reshape(nodes), edge_part.reshape(-1), node_part.reshape(-1)


def solution(mesh):
    placed = (
        P("gx", "gy", None, None),
        P(None, "gx", "gy", None, None),
        P(None, "gx", "gy", None),
        P(),
        P(),
        P("gx", "gy", None, None),
    )
    return jax.shard_map(
        local,
        mesh=mesh,
        in_specs=placed,
        out_specs=(
            P("gx", "gy", None, None),
            P("gx", "gy", None, None),
            P(("gx", "gy")),
            P(("gx", "gy")),
        ),
        check_vma=False,
    )
```
